32 devices in a mesh: seq: 4 (over x, core), clip: 8 (over z, y).
Axes of the slice: x: 2, y: 2, z: 4, core: 2. Of those that a mesh axis runs over, the one named last changes fastest.
Arguments:
- patches: bfloat16 [64, 8, 64, 768], P('clip', None, 'seq'), may hold values from -6 to 6
- mask_index: int32 [64, 450], P('clip'), may hold values from 0 to 511, as said below
- mask_count: int32 [64], P('clip'), may hold values from 100 to 450, as said below
- cotangent: bfloat16 [64, 8, 64, 768], P('clip', None, 'seq'), may hold values from -6 to 6
- w_qkv: bfloat16 [768, 2304], P(('seq', 'clip')), may hold values from -0.3125 to 0.3125
- w_out: bfloat16 [768, 768], P(('seq', 'clip')), may hold values from -0.4375 to 0.4375
- mask_embed: bfloat16 [768], P(('seq', 'clip')), may hold values from -5 to 5
- gains: bfloat16 [2, 768], P(None, ('seq', 'clip')), may hold values from 0.5 to 1.5
- biases: bfloat16 [6, 768], P(None, ('seq', 'clip')), may hold values from -0.5 to 0.5
- w_up: bfloat16 [768, 3072], P(('seq', 'clip')), may hold values from -0.21875 to 0.21875
- w_down: bfloat16 [3072, 768], P(('seq', 'clip')), may hold values from -0.109375 to 0.109375
- up_bias: bfloat16 [3072], P(('seq', 'clip')), may hold values from -2.5 to 2.5
- avg_qkv: float32 [768, 2304], P(('seq', 'clip')), may hold values from -0.3125 to 0.3125
- avg_out: float32 [768, 768], P(('seq', 'clip')), may hold values from -0.4375 to 0.4375
- avg_mask: float32 [768], P(('seq', 'clip')), may hold values from -5 to 5
- avg_gains: float32 [2, 768], P(None, ('seq', 'clip')), may hold values from -1 to 1
- avg_biases: float32 [6, 768], P(None, ('seq', 'clip')), may hold values from -0.5 to 0.5
- avg_up: float32 [768, 3072], P(('seq', 'clip')), may hold values from -0.21875 to 0.21875
- avg_down: float32 [3072, 768], P(('seq', 'clip')), may hold values from -0.109375 to 0.109375
- avg_up_bias: float32 [3072], P(('seq', 'clip')), may hold values from -2.5 to 2.5
Outputs:
- activations: bfloat16 [64, 8, 64, 768], P('clip', None, 'seq')
- input_grad: bfloat16 [64, 8, 64, 768], P('clip', None, 'seq')
- grad_qkv: float32 [768, 2304], P(('seq', 'clip'))
- grad_out: float32 [768, 768], P(('seq', 'clip'))
- grad_mask: float32 [768], P(('seq', 'clip'))
- grad_gains: float32 [2, 768], P(None, ('seq', 'clip'))
- grad_biases: float32 [6, 768], P(None, ('seq', 'clip'))
- grad_up: float32 [768, 3072], P(('seq', 'clip'))
- grad_down: float32 [3072, 768], P(('seq', 'clip'))
- grad_up_bias: float32 [3072], P(('seq', 'clip'))
- new_qkv: float32 [768, 2304], P(('seq', 'clip'))
- new_out: float32 [768, 768], P(('seq', 'clip'))
- new_mask: float32 [768], P(('seq', 'clip'))
- new_gains: float32 [2, 768], P(None, ('seq', 'clip'))
- new_biases: float32 [6, 768], P(None, ('seq', 'clip'))
- new_up: float32 [768, 3072], P(('seq', 'clip'))
- new_down: float32 [3072, 768], P(('seq', 'clip'))
- new_up_bias: float32 [3072], P(('seq', 'clip'))
The draws below stay inside these ranges and needn't reach their ends.
Inputs may be any that keep to these rules, and one draw needn't show every extreme that they name: `mask_index`: each row holds 450 different patch numbers of its clip; only its first mask_count entries are masked, the others are to be ignored. `mask_count`: some clip has exactly 450 masked patches in every draw.
All inputs are finite; a program needn't handle non-finite values.
Results may differ from the reference program's by a relative error of at most 0.015.
Values may be sent and summed in bfloat16 or wider, within the bound.
No kernel may reach another device: no remote copies, remote signals or barrier semaphores. Data moves between devices by JAX's collectives and lax.ppermute only.
A program may use at most 192 MiB of HBM per device.

```python
import math
import jax
import jax.numpy as jnp
from jax import lax

D = 768
H = 12
HD = 64
FF = 3072
FREQ = 8
TIME = 64
MASK_SLOTS = 450
MIN_MASK = 100
CLIPS = 64


def draw_mask_index(key, part):
    clip_keys = jax.random.split(jax.random.fold_in(key, 11), CLIPS)

    def one_clip(clip_key):
        return jax.random.permutation(clip_key, FREQ * TIME)[:MASK_SLOTS]
    return jax.vmap(one_clip)(clip_keys).astype(jnp.int32)


def draw_mask_count(key, part):
    first_key, second_key, third_key = jax.random.split(jax.random.fold_in(key, 23), 3)
    counts = jax.random.randint(first_key, (CLIPS,), MIN_MASK, MASK_SLOTS + 1)
    busiest = jax.random.randint(second_key, (), 0, CLIPS)
    lightest = (busiest + 1 + jax.random.randint(third_key, (), 0, max(CLIPS - 1, 1))) % CLIPS
    counts = counts.at[lightest].set(MIN_MASK)
    counts = counts.at[busiest].set(MASK_SLOTS)
    return counts.astype(jnp.int32)


def spiked(values, key, source, target, parts, factor):
    def block_of(position):
        return (jnp.arange(values.shape[position]) // (values.shape[position] // parts)).reshape((-1,) + (1,) * (values.ndim - 1 - position))

    near = jax.random.permutation(key, parts)[block_of(target)]
    other_side = (block_of(target) + parts // 2) % parts
    return jnp.where((block_of(source) == near) | (block_of(source) == other_side), factor * values, values)


def shard_levels(stream_key, extent, cuts, least, largest):
    def one(dim, shards_of):
        steps = jax.random.uniform(jax.random.fold_in(jax.random.fold_in(stream_key, 6), dim), (shards_of,), jnp.float32, least / len(cuts), largest / len(cuts))
        return jnp.repeat(jnp.exp(steps), extent[dim] // shards_of).reshape((-1,) + (1,) * (len(extent) - dim - 1))

    loudness = one(*cuts[0])
    for cut in cuts[1:]:
        loudness = loudness * one(*cut)
    return loudness


def scatter_about(stream_key, shape, scale, bound, pieces=(), kind=jnp.bfloat16):
    entries = jax.random.normal(stream_key, shape, jnp.float32) * scale
    if len(pieces) > 0:
        entries = shard_levels(stream_key, shape, pieces, -0.22, 0.18) * entries
    return jnp.clip(entries, min=-bound, max=bound).astype(kind)


def bell_draw_with(own_key, dims, scale, most, pieces, heavy, kind=jnp.bfloat16):
    values = scale * jax.random.normal(own_key, dims, jnp.float32)
    if pieces:
        values = values * shard_levels(own_key, dims, pieces, -0.22, 0.18)
    return jnp.clip(spiked(values, jax.random.fold_in(own_key, 3), *heavy), -most, most).astype(kind)


def setup_inputs(seed: int = 0) -> dict:
    arg_keys = jax.random.split(jax.random.key(seed), 21)
    return {
        "patches": scatter_about(arg_keys[0], (CLIPS, FREQ, TIME, D), 1.0, 6.0, ((0, 8), (2, 4))),
        "mask_index": draw_mask_index(jax.random.fold_in(arg_keys[20], 71), 0),
        "mask_count": draw_mask_count(jax.random.fold_in(arg_keys[20], 71), 0),
        "cotangent": bell_draw_with(arg_keys[3], (CLIPS, FREQ, TIME, D), 1.0, 6.0, ((0, 8), (2, 4)), (0, 3, 8, 2.0)),
        "w_qkv": scatter_about(arg_keys[4], (D, 3 * D), (D // 2) ** -0.5, 0.3125, ((0, 32),)),
        "w_out": scatter_about(arg_keys[5], (D, D), (D // 4) ** -0.5, 0.4375, ((0, 32),)),
        "mask_embed": scatter_about(arg_keys[6], (D,), 1.0, 5.0, ((0, 32),)),
        "gains": jnp.clip(1.0 + 0.1 * jax.random.normal(arg_keys[7], (2, D), jnp.float32), 0.5, 1.5).astype(jnp.bfloat16),
        "biases": scatter_about(arg_keys[8], (6, D), 0.1, 0.5, ((1, 32),)),
        "w_up": scatter_about(arg_keys[9], (D, FF), D ** -0.5, 0.21875, ((0, 32),)),
        "w_down": scatter_about(arg_keys[10], (FF, D), FF ** -0.5, 0.109375, ((0, 32),)),
        "up_bias": scatter_about(arg_keys[11], (FF,), 0.5, 2.5, ((0, 32),)),
        "avg_qkv": scatter_about(arg_keys[12], (D, 3 * D), (D // 2) ** -0.5, 0.3125, ((0, 32),), jnp.float32),
        "avg_out": scatter_about(arg_keys[13], (D, D), (D // 4) ** -0.5, 0.4375, ((0, 32),), jnp.float32),
        "avg_mask": scatter_about(arg_keys[14], (D,), 1.0, 5.0, ((0, 32),), jnp.float32),
        "avg_gains": jnp.clip(jax.random.uniform(arg_keys[15], (2, D), jnp.float32, -1.0, 1.0) * shard_levels(arg_keys[15], (2, D), ((1, 32),), -0.4, 0.0), -1.0, 1.0),
        "avg_biases": scatter_about(arg_keys[16], (6, D), 0.1, 0.5, ((1, 32),), jnp.float32),
        "avg_up": scatter_about(arg_keys[17], (D, FF), D ** -0.5, 0.21875, ((0, 32),), jnp.float32),
        "avg_down": scatter_about(arg_keys[18], (FF, D), FF ** -0.5, 0.109375, ((0, 32),), jnp.float32),
        "avg_up_bias": scatter_about(arg_keys[19], (FF,), 0.5, 2.5, ((0, 32),), jnp.float32),
    }


norm_eps = 1e-06
highest = lax.Precision.HIGHEST

@jax.custom_vjp
def low(v):
    return lax.optimization_barrier(v.astype(jnp.bfloat16)).astype(jnp.float32)

@jax.custom_vjp
def low_back(v):
    return v

def low_keep(v):
    return (low(v), None)

def low_pass(kept, grad):
    return (grad,)

def back_keep(v):
    return (v, None)

def back_low(kept, grad):
    return (low(grad),)
low.defvjp(low_keep, low_pass)
low_back.defvjp(back_keep, back_low)

def layer_norm(hidden, gain_row, shift_row):
    center = hidden - lax.optimization_barrier(jnp.mean(hidden, axis=-1, keepdims=True))
    spread = lax.optimization_barrier(jnp.mean(center * center, axis=-1, keepdims=True))
    return center * lax.rsqrt(spread + norm_eps) * gain_row + shift_row

def matmul(left_side, right_side):
    return jnp.matmul(left_side, right_side, precision=highest)

def attend_clip(queries, keys_all, values_all):
    length = queries.shape[0]
    query_h = queries.reshape(length, H, HD)
    key_h = keys_all.reshape(length, H, HD)
    value_h = values_all.reshape(length, H, HD)
    scores = jnp.einsum('qhd,khd->hqk', query_h, key_h, precision=highest) * (1.0 / math.sqrt(HD))
    scores = low_back(scores)
    shifted = jnp.exp(scores - lax.optimization_barrier(jnp.max(scores, axis=-1, keepdims=True)))
    attn_prob = shifted / lax.optimization_barrier(jnp.sum(shifted, axis=-1, keepdims=True))
    mixed_rows = jnp.einsum('hqk,khd->qhd', low(attn_prob), value_h, precision=highest)
    return mixed_rows.reshape(length, H * HD)

def attend_pack(operands):
    return attend_clip(operands[0], operands[1], operands[2])

def block_forward(block_in, masked, w_qkv, w_out, mask_embed, gains, biases, w_up, w_down, up_bias):
    width = H * HD
    start_rows = jnp.where(masked[..., None], mask_embed, block_in)
    normed = low(layer_norm(start_rows, gains[0], biases[0]))
    joined = matmul(normed, w_qkv)
    queries = low(low_back(joined[..., :width] + biases[1]))
    keys_all = low(low_back(joined[..., width:2 * width]))
    values_all = low(low_back(joined[..., 2 * width:] + biases[2]))
    mixed_rows = lax.map(jax.checkpoint(attend_pack), (queries, keys_all, values_all))
    mixed_rows = low(low_back(mixed_rows))
    middle = start_rows + low_back(matmul(mixed_rows, w_out) + biases[3])
    second = low(layer_norm(middle, gains[1], biases[4]))
    upper_rows = low_back(matmul(second, w_up) + up_bias)
    active = low(jax.nn.gelu(upper_rows, approximate=False))
    return middle + low_back(matmul(active, w_down) + biases[5])

def reference(patches, mask_index, mask_count, cotangent, w_qkv, w_out, mask_embed, gains, biases, w_up, w_down, up_bias, avg_qkv, avg_out, avg_mask, avg_gains, avg_biases, avg_up, avg_down, avg_up_bias):
    params = tuple((param_item.astype(jnp.float32) for param_item in (w_qkv, w_out, mask_embed, gains, biases, w_up, w_down, up_bias)))
    length = FREQ * TIME
    width = H * HD
    group_size = math.gcd(CLIPS, max(1, 4096 // length))
    steps_count = CLIPS // group_size
    flat_in = patches.astype(jnp.float32).reshape(steps_count, group_size, length, width)
    flat_cot = cotangent.astype(jnp.float32).reshape(steps_count, group_size, length, width)
    index_rows = mask_index.astype(jnp.int32).reshape(steps_count, group_size, MASK_SLOTS)
    count_rows = mask_count.astype(jnp.int32).reshape(steps_count, group_size)
    positions = jnp.arange(length, dtype=jnp.int32)
    slot_ids = jnp.arange(MASK_SLOTS, dtype=jnp.int32)

    def step_fn(totals, inputs):
        block_in, block_cot, block_index, block_count = inputs
        slot_live = slot_ids[None, :] < block_count[:, None]
        slot_hits = (block_index[:, :, None] == positions[None, None, :]) & slot_live[:, :, None]
        masked = jnp.any(slot_hits, axis=1)

        def run_block(block_rows, *weights):
            return block_forward(block_rows, masked, *weights)
        result, pull_back = jax.vjp(run_block, block_in, *params)
        grad_list = pull_back(block_cot)
        totals = tuple((total_item + extra_item for total_item, extra_item in zip(totals, grad_list[1:])))
        return (totals, (result.astype(jnp.bfloat16), grad_list[0].astype(jnp.bfloat16)))
    init = tuple((jnp.zeros(param_item.shape, jnp.float32) for param_item in params))
    totals, outputs = lax.scan(step_fn, init, (flat_in, flat_cot, index_rows, count_rows))
    activations = outputs[0].reshape(CLIPS, FREQ, TIME, width)
    input_grad = outputs[1].reshape(CLIPS, FREQ, TIME, width)
    averages = (avg_qkv, avg_out, avg_mask, avg_gains, avg_biases, avg_up, avg_down, avg_up_bias)
    news = tuple((0.9 * avg_item + 0.1 * param_item for avg_item, param_item in zip(averages, params)))
    return (activations, input_grad, totals[0], totals[1], totals[2], totals[3], totals[4], totals[5], totals[6], totals[7], news[0], news[1], news[2], news[3], news[4], news[5], news[6], news[7])
```

```python
import math
from functools import partial

import jax
import jax.numpy as jnp
from jax import lax
from jax.experimental import pallas as pl
from jax.experimental.pallas import tpu as pltpu
from jax.sharding import Mesh, PartitionSpec as P

H = 12
norm_eps = 1e-06
F32 = jnp.float32
BF16 = jnp.bfloat16
ALL = ("sx", "core", "clip")


def layer_norm(hidden, gain_row, shift_row):
    center = hidden - jnp.mean(hidden, axis=-1, keepdims=True)
    spread = jnp.mean(center * center, axis=-1, keepdims=True)
    return center * lax.rsqrt(spread + norm_eps) * gain_row + shift_row


def exact_gelu(upper_rows):
    return upper_rows * (0.5 + 0.5 * lax.erf(upper_rows * math.sqrt(0.5)))


def dot(left_side, right_side, left_dim, right_dim):
    return lax.dot_general(
        left_side, right_side, (((left_dim,), (right_dim,)), ((), ())), preferred_element_type=F32
    )


def forward_kernel(q_ref, k_ref, v_ref, o_ref, log_ref, *, head_size, scale):
    length = q_ref.shape[0] * q_ref.shape[2]
    query = q_ref[...].reshape(length, -1) * scale
    key = k_ref[...].reshape(length, -1)
    value = v_ref[...].reshape(length, -1)
    mixed = []
    for i in range(query.shape[1] // head_size):
        cols = slice(i * head_size, (i + 1) * head_size)
        scores = dot(key[:, cols], query[:, cols], 1, 1)
        top = jnp.max(scores, axis=0, keepdims=True)
        shifted = jnp.exp(scores - top)
        total = jnp.sum(shifted, axis=0, keepdims=True)
        mixed.append(dot(value[:, cols], shifted.astype(BF16), 0, 0) / total)
        log_ref[0, 0, i : i + 1, :] = top + jnp.log(total)
    mixed = jnp.concatenate(mixed, axis=0).T.astype(BF16)
    o_ref[...] = mixed.reshape(o_ref.shape)


def backward_kernel(q_ref, k_ref, v_ref, g_ref, log_ref, dq_ref, dk_ref, dv_ref, *, head_size, scale):
    length = q_ref.shape[0] * q_ref.shape[2]
    query = q_ref[...].reshape(length, -1) * scale
    key = k_ref[...].reshape(length, -1)
    value = v_ref[...].reshape(length, -1)
    grad = g_ref[...].reshape(length, -1)
    grad_query, grad_key, grad_value = [], [], []
    for i in range(query.shape[1] // head_size):
        cols = slice(i * head_size, (i + 1) * head_size)
        scores = dot(key[:, cols], query[:, cols], 1, 1)
        prob = jnp.exp(scores - log_ref[0, 0, i : i + 1, :])
        grad_prob = dot(value[:, cols], grad[:, cols], 1, 1)
        inner = jnp.sum(grad_prob * prob, axis=0, keepdims=True)
        grad_scores = (prob * (grad_prob - inner)).astype(BF16)
        grad_query.append(dot(key[:, cols], grad_scores, 0, 0))
        grad_key.append(dot(grad_scores, query[:, cols], 1, 0))
        grad_value.append(dot(prob.astype(BF16), grad[:, cols], 1, 0))
    dq = (jnp.concatenate(grad_query, axis=0) * scale).T.astype(BF16)
    dq_ref[...] = dq.reshape(dq_ref.shape)
    dk_ref[...] = jnp.concatenate(grad_key, axis=1).astype(BF16).reshape(dk_ref.shape)
    dv_ref[...] = jnp.concatenate(grad_value, axis=1).astype(BF16).reshape(dv_ref.shape)


def head_spec(shape, offset):
    slots, _, rows, _ = shape
    return pl.BlockSpec((slots, 1, rows, 128), lambda c, j: (0, c, 0, j + offset))


def attend_forward(queries, keys, values, head_count):
    slots, clips, rows, width = queries.shape
    head_size = width // head_count
    blocks, per_block = width // 128, 128 // head_size
    return pl.pallas_call(
        partial(forward_kernel, head_size=head_size, scale=1.0 / math.sqrt(head_size)),
        grid=(clips, blocks),
        in_specs=[head_spec(queries.shape, 0)] * 3,
        out_specs=[
            head_spec(queries.shape, 0),
            pl.BlockSpec((1, 1, per_block, slots * rows), lambda c, j: (c, j, 0, 0)),
        ],
        out_shape=[
            jax.ShapeDtypeStruct(queries.shape, BF16),
            jax.ShapeDtypeStruct((clips, blocks, per_block, slots * rows), F32),
        ],
        name="attend_forward",
    )(queries, keys, values)


def attend_backward(queries, keys, values, grad_mixed, logs, head_count, first, count):
    slots, clips, rows, width = queries.shape
    head_size = width // head_count
    per_block = 128 // head_size
    spec = head_spec(queries.shape, first)
    out_spec = head_spec(queries.shape, 0)
    out_shape = jax.ShapeDtypeStruct((slots, clips, rows, count * 128), BF16)
    return pl.pallas_call(
        partial(backward_kernel, head_size=head_size, scale=1.0 / math.sqrt(head_size)),
        grid=(clips, count),
        in_specs=[spec] * 4
        + [pl.BlockSpec((1, 1, per_block, slots * rows), lambda c, j: (c, j + first, 0, 0))],
        out_specs=[out_spec] * 3,
        out_shape=[out_shape] * 3,
        name="attend_backward",
    )(queries, keys, values, grad_mixed, logs)


def swap(array, axis_name, bit):
    size = lax.axis_size(axis_name)
    return lax.ppermute(array, axis_name, [(i, i ^ bit) for i in range(size)])


def bit_of(axis_name, bit):
    return (lax.axis_index(axis_name) // bit) % 2


def device_bits():
    bits = []
    for axis_name in ALL:
        bit = lax.axis_size(axis_name) // 2
        while bit:
            bits.append((axis_name, bit))
            bit //= 2
    return bits


def scatter_sum(part, order, send_type=BF16):
    left = device_bits()
    array = part.reshape((2,) * len(left) + part.shape[1:])
    for step in order:
        axis = left.index(step)
        mine = bit_of(*step)
        keep = lax.dynamic_index_in_dim(array, mine, axis, False)
        send = lax.dynamic_index_in_dim(array, 1 - mine, axis, False).astype(send_type)
        array = keep + swap(send, *step).astype(F32)
        left.pop(axis)
    return array


def gather_all(shard, order):
    bits = device_bits()
    array, have = shard, []
    for step in order:
        other = swap(array, *step)
        have = sorted(have + [step], key=bits.index)
        axis = have.index(step)
        mine = bit_of(*step)
        both = jnp.stack([array, other], axis=axis)
        flip = jnp.stack([other, array], axis=axis)
        array = jnp.where(mine == 0, both, flip)
    return array.reshape((-1,) + shard.shape)


def body(
    patches,
    mask_index,
    mask_count,
    cotangent,
    w_qkv,
    w_out,
    mask_embed,
    gains,
    biases,
    w_up,
    w_down,
    up_bias,
    avg_qkv,
    avg_out,
    avg_mask,
    avg_gains,
    avg_biases,
    avg_up,
    avg_down,
    avg_up_bias,
):
    clip_count, freq_rows, time_local, width = patches.shape
    seq_names = ("sx", "core")
    seq_size = lax.axis_size("sx") * lax.axis_size("core")
    seq_here = lax.axis_index(seq_names)
    devices = seq_size * lax.axis_size("clip")
    local_len = freq_rows * time_local
    own_clips = clip_count // seq_size
    row_total = seq_size * own_clips * local_len
    grid_shape = (seq_size, own_clips, local_len, width)

    bits = device_bits()
    clip_bits = [b for b in bits if b[0] == "clip"]
    other_bits = [b for b in bits if b[0] == "sx"]
    core_bits = [b for b in bits if b[0] == "core"]
    low_first = clip_bits[::-1]
    order_a = core_bits + other_bits + low_first
    order_b = core_bits + low_first[:1] + other_bits + low_first[1:]

    def trade(chunks):
        return [chunks[0]] + [
            lax.ppermute(chunks[k], seq_names, [(i, i ^ k) for i in range(seq_size)])
            for k in range(1, seq_size)
        ]

    def rows_in(array):
        array = array.reshape(seq_size, own_clips, local_len, width)
        got = trade(
            [lax.dynamic_index_in_dim(array, seq_here ^ k, 0, False) for k in range(seq_size)]
        )
        return jnp.stack(got).reshape(row_total, width)

    def rows_out(array):
        array = array.reshape(grid_shape)
        got = jnp.stack(trade([array[k] for k in range(seq_size)]))
        order = [lax.dynamic_index_in_dim(got, seq_here ^ k, 0, False) for k in range(seq_size)]
        return jnp.stack(order).reshape(patches.shape)

    share = width // devices
    up_share = up_bias.shape[0]
    small = jnp.concatenate([mask_embed, gains.reshape(-1), biases.reshape(-1), up_bias])
    small_size = small.shape[0]
    small_padded = -(-small_size // 128) * 128
    small = jnp.pad(small, (0, small_padded - small_size))
    small_all = gather_all(small, clip_bits + other_bits + core_bits)

    full_qkv = lax.all_gather(w_qkv, ALL, axis=0, tiled=True)
    patch_rows = rows_in(patches)
    grad_final = rows_in(cotangent)
    full_out = lax.all_gather(w_out, ALL, axis=0, tiled=True)
    full_up = lax.all_gather(w_up, ALL, axis=0, tiled=True)
    full_down = lax.all_gather(w_down, ALL, axis=0, tiled=True)

    small_rows = small_all[:, : 9 * share].astype(F32).reshape(devices, 9, share)
    small_rows = small_rows.transpose(1, 0, 2).reshape(9, width)
    mask_vector, gain_rows, bias_rows = small_rows[0], small_rows[1:3], small_rows[3:9]
    up_shift = small_all[:, 9 * share : small_size].astype(F32).reshape(-1)

    slot_ids = lax.broadcasted_iota(jnp.int32, (seq_size, freq_rows, time_local), 0)
    freq_ids = lax.broadcasted_iota(jnp.int32, (seq_size, freq_rows, time_local), 1)
    time_ids = lax.broadcasted_iota(jnp.int32, (seq_size, freq_rows, time_local), 2)
    time_ids = time_ids + (slot_ids ^ seq_here) * time_local
    positions = (freq_ids * (time_local * seq_size) + time_ids).reshape(-1)
    own_index = lax.dynamic_slice_in_dim(mask_index, seq_here * own_clips, own_clips, 0)
    own_count = lax.dynamic_slice_in_dim(mask_count, seq_here * own_clips, own_clips, 0)
    live = lax.broadcasted_iota(jnp.int32, own_index.shape, 1) < own_count[:, None]
    live_index = jnp.where(live, own_index, -1)
    hits = live_index[:, :, None] == positions[None, None, :]
    masked = jnp.any(hits, axis=1).reshape(own_clips, seq_size, local_len)
    masked = masked.transpose(1, 0, 2).reshape(row_total, 1)

    start_rows = jnp.where(masked, mask_vector, patch_rows.astype(F32))
    normed_one, norm_pull_one = jax.vjp(layer_norm, start_rows, gain_rows[0], bias_rows[0])
    normed_low = normed_one.astype(BF16)
    joined = jnp.dot(normed_low, full_qkv, preferred_element_type=F32)
    queries = (joined[:, :width] + bias_rows[1]).astype(BF16).reshape(grid_shape)
    keys = joined[:, width : 2 * width].astype(BF16).reshape(grid_shape)
    values = (joined[:, 2 * width :] + bias_rows[2]).astype(BF16).reshape(grid_shape)
    mixed, logs = attend_forward(queries, keys, values, H)
    mixed_flat = mixed.reshape(row_total, width)
    middle = start_rows + (jnp.dot(mixed_flat, full_out, preferred_element_type=F32) + bias_rows[3])
    normed_two, norm_pull_two = jax.vjp(layer_norm, middle, gain_rows[1], bias_rows[4])
    second_low = normed_two.astype(BF16)
    upper_rows = jnp.dot(second_low, full_up, preferred_element_type=F32) + up_shift
    active, gelu_pull = jax.vjp(exact_gelu, upper_rows)
    active_low = active.astype(BF16)
    final_rows = middle + (jnp.dot(active_low, full_down, preferred_element_type=F32) + bias_rows[5])
    activations = rows_out(final_rows.astype(BF16))

    def by_owner(part):
        return part.reshape(devices, -1, part.shape[1])

    def send_grad(part):
        half = part.shape[1] // 2
        part = by_owner(part)
        return jnp.concatenate(
            [scatter_sum(part[..., :half], order_a), scatter_sum(part[..., half:], order_b)], axis=1
        )

    grad_down = send_grad(dot(active_low, grad_final, 0, 0))
    grad_down_bias = jnp.sum(grad_final.astype(F32), axis=0)
    grad_active = dot(grad_final, full_down, 1, 1)
    (grad_upper,) = gelu_pull(grad_active)
    grad_upper_low = grad_upper.astype(BF16)
    grad_up = send_grad(dot(second_low, grad_upper_low, 0, 0))
    grad_up_shift = jnp.sum(grad_upper_low.astype(F32), axis=0)
    grad_second = dot(grad_upper_low, full_up, 1, 1)
    grad_mid_norm, grad_gain_two, grad_bias_two = norm_pull_two(grad_second)
    grad_middle = grad_final.astype(F32) + grad_mid_norm
    grad_branch = grad_middle.astype(BF16)
    grad_out = send_grad(dot(mixed_flat, grad_branch, 0, 0))
    grad_out_bias = jnp.sum(grad_branch.astype(F32), axis=0)
    grad_mixed = dot(grad_branch, full_out, 1, 1).astype(BF16).reshape(grid_shape)
    groups = 3
    per_group = width // 128 // groups
    pieces = [
        attend_backward(queries, keys, values, grad_mixed, logs, H, g * per_group, per_group)
        for g in range(groups)
    ]
    grad_joined = jnp.concatenate(
        [p[i].reshape(row_total, -1) for i in range(3) for p in pieces], axis=1
    )
    grad_qkv = send_grad(dot(normed_low, grad_joined, 0, 0))
    grad_query_bias = jnp.sum(grad_joined[:, :width].astype(F32), axis=0)
    grad_value_bias = jnp.sum(grad_joined[:, 2 * width :].astype(F32), axis=0)
    grad_first = dot(grad_joined, full_qkv, 1, 1)
    grad_start_norm, grad_gain_one, grad_bias_one = norm_pull_one(grad_first)
    grad_start = grad_middle + grad_start_norm
    input_grad = rows_out(jnp.where(masked, 0.0, grad_start).astype(BF16))
    grad_mask_part = jnp.sum(jnp.where(masked, grad_start, 0.0), axis=0)
    small_grads = jnp.stack(
        [
            grad_mask_part,
            grad_gain_one,
            grad_gain_two,
            grad_bias_one,
            grad_query_bias,
            grad_value_bias,
            grad_out_bias,
            grad_bias_two,
            grad_down_bias,
        ]
    )
    small_grads = small_grads.reshape(9, devices, share).transpose(1, 0, 2).reshape(devices, -1)
    small_grads = jnp.concatenate([small_grads, grad_up_shift.reshape(devices, up_share)], axis=1)
    small_grads = jnp.pad(small_grads, ((0, 0), (0, small_padded - small_size)))
    small_sum = scatter_sum(small_grads, order_a, F32)
    own_rows = small_sum[: 9 * share].reshape(9, share)

    def moved(average, param):
        return 0.9 * average + 0.1 * param.astype(F32)

    return (
        activations,
        input_grad,
        grad_qkv,
        grad_out,
        own_rows[0],
        own_rows[1:3],
        own_rows[3:9],
        grad_up,
        grad_down,
        small_sum[9 * share : small_size],
        moved(avg_qkv, w_qkv),
        moved(avg_out, w_out),
        moved(avg_mask, mask_embed),
        moved(avg_gains, gains),
        moved(avg_biases, biases),
        moved(avg_up, w_up),
        moved(avg_down, w_down),
        moved(avg_up_bias, up_bias),
    )


def solution(mesh):
    seq_size, clip_size = mesh.shape["seq"], mesh.shape["clip"]
    fine = Mesh(mesh.devices.reshape(seq_size // 2, 2, clip_size), ALL)
    rows = P("clip", None, ("sx", "core"), None)
    first, second, only = P(ALL, None), P(None, ALL), P(ALL)
    params = (first, first, only, second, second, first, first, only)
    return jax.shard_map(
        body,
        mesh=fine,
        in_specs=(rows, P("clip", None), P("clip"), rows) + params + params,
        out_specs=(rows, rows) + params + params,
        check_vma=False,
    )
```

```python
import math
from functools import partial

import jax
import jax.numpy as jnp
from jax import lax
from jax.experimental import pallas as pl
from jax.experimental.pallas import tpu as pltpu
from jax.sharding import Mesh, PartitionSpec as P

H = 12
norm_eps = 1e-06
F32 = jnp.float32
BF16 = jnp.bfloat16
ALL = ("sx", "core", "clip")


def layer_norm(hidden, gain_row, shift_row):
    center = hidden - jnp.mean(hidden, axis=-1, keepdims=True)
    spread = jnp.mean(center * center, axis=-1, keepdims=True)
    return center * lax.rsqrt(spread + norm_eps) * gain_row + shift_row


def exact_gelu(upper_rows):
    return upper_rows * (0.5 + 0.5 * lax.erf(upper_rows * math.sqrt(0.5)))


def dot(left_side, right_side, left_dim, right_dim):
    return lax.dot_general(
        left_side, right_side, (((left_dim,), (right_dim,)), ((), ())), preferred_element_type=F32
    )


def forward_kernel(q_ref, k_ref, v_ref, o_ref, log_ref, *, head_size, scale):
    length = q_ref.shape[0] * q_ref.shape[2]
    query = q_ref[...].reshape(length, -1) * scale
    key = k_ref[...].reshape(length, -1)
    value = v_ref[...].reshape(length, -1)
    mixed = []
    for i in range(query.shape[1] // head_size):
        cols = slice(i * head_size, (i + 1) * head_size)
        scores = dot(key[:, cols], query[:, cols], 1, 1)
        top = jnp.max(scores, axis=0, keepdims=True)
        shifted = jnp.exp(scores - top)
        total = jnp.sum(shifted, axis=0, keepdims=True)
        mixed.append(dot(value[:, cols], shifted.astype(BF16), 0, 0) / total)
        log_ref[0, 0, i : i + 1, :] = top + jnp.log(total)
    mixed = jnp.concatenate(mixed, axis=0).T.astype(BF16)
    o_ref[...] = mixed.reshape(o_ref.shape)


def backward_kernel(q_ref, k_ref, v_ref, g_ref, log_ref, dq_ref, dk_ref, dv_ref, *, head_size, scale):
    length = q_ref.shape[0] * q_ref.shape[2]
    query = q_ref[...].reshape(length, -1) * scale
    key = k_ref[...].reshape(length, -1)
    value = v_ref[...].reshape(length, -1)
    grad = g_ref[...].reshape(length, -1)
    grad_query, grad_key, grad_value = [], [], []
    for i in range(query.shape[1] // head_size):
        cols = slice(i * head_size, (i + 1) * head_size)
        scores = dot(key[:, cols], query[:, cols], 1, 1)
        prob = jnp.exp(scores - log_ref[0, 0, i : i + 1, :])
        grad_prob = dot(value[:, cols], grad[:, cols], 1, 1)
        inner = jnp.sum(grad_prob * prob, axis=0, keepdims=True)
        grad_scores = (prob * (grad_prob - inner)).astype(BF16)
        grad_query.append(dot(key[:, cols], grad_scores, 0, 0))
        grad_key.append(dot(grad_scores, query[:, cols], 1, 0))
        grad_value.append(dot(prob.astype(BF16), grad[:, cols], 1, 0))
    dq = (jnp.concatenate(grad_query, axis=0) * scale).T.astype(BF16)
    dq_ref[...] = dq.reshape(dq_ref.shape)
    dk_ref[...] = jnp.concatenate(grad_key, axis=1).astype(BF16).reshape(dk_ref.shape)
    dv_ref[...] = jnp.concatenate(grad_value, axis=1).astype(BF16).reshape(dv_ref.shape)


def head_spec(shape, offset):
    slots, _, rows, _ = shape
    return pl.BlockSpec((slots, 1, rows, 128), lambda c, j: (0, c, 0, j + offset))


def attend_forward(queries, keys, values, head_count):
    slots, clips, rows, width = queries.shape
    head_size = width // head_count
    blocks, per_block = width // 128, 128 // head_size
    return pl.pallas_call(
        partial(forward_kernel, head_size=head_size, scale=1.0 / math.sqrt(head_size)),
        grid=(clips, blocks),
        in_specs=[head_spec(queries.shape, 0)] * 3,
        out_specs=[
            head_spec(queries.shape, 0),
            pl.BlockSpec((1, 1, per_block, slots * rows), lambda c, j: (c, j, 0, 0)),
        ],
        out_shape=[
            jax.ShapeDtypeStruct(queries.shape, BF16),
            jax.ShapeDtypeStruct((clips, blocks, per_block, slots * rows), F32),
        ],
        name="attend_forward",
    )(queries, keys, values)


def attend_backward(queries, keys, values, grad_mixed, logs, head_count, first, count):
    slots, clips, rows, width = queries.shape
    head_size = width // head_count
    per_block = 128 // head_size
    spec = head_spec(queries.shape, first)
    out_spec = head_spec(queries.shape, 0)
    out_shape = jax.ShapeDtypeStruct((slots, clips, rows, count * 128), BF16)
    return pl.pallas_call(
        partial(backward_kernel, head_size=head_size, scale=1.0 / math.sqrt(head_size)),
        grid=(clips, count),
        in_specs=[spec] * 4
        + [pl.BlockSpec((1, 1, per_block, slots * rows), lambda c, j: (c, j + first, 0, 0))],
        out_specs=[out_spec] * 3,
        out_shape=[out_shape] * 3,
        name="attend_backward",
    )(queries, keys, values, grad_mixed, logs)


def after(array, *earlier):
    return lax.optimization_barrier((array,) + earlier)[0]


def device_bits():
    bits = []
    for axis_name in ALL:
        bit = lax.axis_size(axis_name) // 2
        while bit:
            bits.append((axis_name, bit))
            bit //= 2
    return bits


def make_stages(bits):
    core = [b for b in bits if b[0] == "core"]
    clip = [b for b in bits if b[0] == "clip"][::-1]
    plane = [b for b in bits if b[0] == "sx"] + clip[:1]
    stages = [core, plane] + [clip[i : i + 2] for i in range(1, len(clip), 2)]
    return [sorted(stage, key=bits.index) for stage in stages]


def partners(stage):
    count = len(stage)
    return [[(k >> i) & 1 for i in range(count)] for k in range(1, 1 << count)]


def send_to(array, stage, flags):
    axes = tuple(dict.fromkeys(step[0] for step in stage))
    sizes = [lax.axis_size(name) for name in axes]
    flip = [sum(s[1] for s, f in zip(stage, flags) if f and s[0] == name) for name in axes]
    total = math.prod(sizes)
    if len(axes) == 1:
        return lax.ppermute(array, axes[0], [(i, i ^ flip[0]) for i in range(total)])
    pairs = [(i, (i // sizes[1] ^ flip[0]) * sizes[1] + (i % sizes[1] ^ flip[1])) for i in range(total)]
    return lax.ppermute(array, axes, pairs)


def own_bit(step):
    return (lax.axis_index(step[0]) // step[1]) % 2


class Reduction:
    def __init__(self, part, send_type=BF16):
        self.left = device_bits()
        self.stages = make_stages(self.left)
        self.array = part.reshape((2,) * len(self.left) + part.shape[1:])
        self.send_type = send_type

    def pick(self, array, stage, flags):
        left = list(self.left)
        for step, flag in zip(stage, flags):
            axis = left.index(step)
            array = lax.dynamic_index_in_dim(array, own_bit(step) ^ flag, axis, False)
            left.pop(axis)
        return array

    def send(self):
        stage = self.stages.pop(0)
        sent = [self.pick(self.array, stage, f).astype(self.send_type) for f in partners(stage)]
        self.array = self.pick(self.array, stage, [0] * len(stage))
        self.left = [step for step in self.left if step not in stage]
        self.got = [send_to(array, stage, f) for array, f in zip(sent, partners(stage))]
        return sent

    def add(self, *earlier):
        got = self.got
        if earlier:
            got = lax.optimization_barrier(tuple(got) + earlier)[: len(got)]
        for array in got:
            self.array = self.array + array.astype(F32)


def gather_all(shard):
    bits = device_bits()
    array, have = shard, []
    for stage in make_stages(bits)[::-1]:
        blocks = [([0] * len(stage), array)]
        blocks += [(f, send_to(array, stage, f)) for f in partners(stage)]
        have = sorted(have + stage, key=bits.index)
        axes = [have.index(step) for step in stage]
        array = jnp.expand_dims(array, axes)
        shape = tuple(2 if i in axes else 1 for i in range(array.ndim))
        for flags, block in blocks[1:]:
            here = jnp.full(shape, True)
            for step, flag, axis in zip(stage, flags, axes):
                here &= lax.broadcasted_iota(jnp.int32, shape, axis) == (own_bit(step) ^ flag)
            array = jnp.where(here, jnp.expand_dims(block, axes), array)
    return array.reshape((-1,) + shard.shape)


def body(
    patches,
    mask_index,
    mask_count,
    cotangent,
    w_qkv,
    w_out,
    mask_embed,
    gains,
    biases,
    w_up,
    w_down,
    up_bias,
    avg_qkv,
    avg_out,
    avg_mask,
    avg_gains,
    avg_biases,
    avg_up,
    avg_down,
    avg_up_bias,
):
    clip_count, freq_rows, time_local, width = patches.shape
    seq_names = ("sx", "core")
    seq_size = lax.axis_size("sx") * lax.axis_size("core")
    seq_here = lax.axis_index(seq_names)
    devices = seq_size * lax.axis_size("clip")
    local_len = freq_rows * time_local
    own_clips = clip_count // seq_size
    row_total = seq_size * own_clips * local_len
    grid_shape = (seq_size, own_clips, local_len, width)

    def trade(chunks):
        return [chunks[0]] + [
            lax.ppermute(chunks[k], seq_names, [(i, i ^ k) for i in range(seq_size)])
            for k in range(1, seq_size)
        ]

    def rows_in(array):
        array = array.reshape(seq_size, own_clips, local_len, width)
        got = trade(
            [lax.dynamic_index_in_dim(array, seq_here ^ k, 0, False) for k in range(seq_size)]
        )
        return jnp.stack(got).reshape(row_total, width)

    def rows_out(array):
        array = array.reshape(grid_shape)
        got = jnp.stack(trade([array[k] for k in range(seq_size)]))
        order = [lax.dynamic_index_in_dim(got, seq_here ^ k, 0, False) for k in range(seq_size)]
        return jnp.stack(order).reshape(patches.shape)

    share = w_qkv.shape[0]
    spread = up_bias.shape[0] // share
    small = jnp.concatenate([mask_embed[None], gains, biases, up_bias.reshape(spread, share)], axis=0)
    small = jnp.pad(small, ((0, 128 - small.shape[0]), (0, 0))).T
    patch_rows = rows_in(patches)
    first_all = gather_all(jnp.concatenate([w_qkv, small], axis=1)).reshape(width, -1)
    full_qkv = first_all[:, : 3 * width]
    small_rows = first_all[:, 3 * width :].astype(F32).T
    mask_vector, gain_rows, bias_rows = small_rows[0], small_rows[1:3], small_rows[3:9]
    up_shift = small_rows[9 : 9 + spread].reshape(spread, devices, share)
    up_shift = up_shift.transpose(1, 0, 2).reshape(-1)

    others = [w_out] + [w_up[:, j * width : (j + 1) * width] for j in range(spread)] + [w_down]
    others_all = lax.all_gather(jnp.concatenate(others, axis=0), ALL, axis=0)

    def other_rows(block):
        return others_all[:, block * share : (block + 1) * share].reshape(width, width)

    full_out = other_rows(0)
    full_up = jnp.concatenate([other_rows(1 + j) for j in range(spread)], axis=1)
    full_down = others_all[:, (1 + spread) * share :].reshape(spread * width, width)

    slot_ids = lax.broadcasted_iota(jnp.int32, (seq_size, freq_rows, time_local), 0)
    freq_ids = lax.broadcasted_iota(jnp.int32, (seq_size, freq_rows, time_local), 1)
    time_ids = lax.broadcasted_iota(jnp.int32, (seq_size, freq_rows, time_local), 2)
    time_ids = time_ids + (slot_ids ^ seq_here) * time_local
    positions = (freq_ids * (time_local * seq_size) + time_ids).reshape(-1)
    own_index = lax.dynamic_slice_in_dim(mask_index, seq_here * own_clips, own_clips, 0)
    own_count = lax.dynamic_slice_in_dim(mask_count, seq_here * own_clips, own_clips, 0)
    live = lax.broadcasted_iota(jnp.int32, own_index.shape, 1) < own_count[:, None]
    live_index = jnp.where(live, own_index, -1)
    hits = live_index[:, :, None] == positions[None, None, :]
    masked = jnp.any(hits, axis=1).reshape(own_clips, seq_size, local_len)
    masked = masked.transpose(1, 0, 2).reshape(row_total, 1)

    start_rows = jnp.where(masked, mask_vector, patch_rows.astype(F32))
    normed_one, norm_pull_one = jax.vjp(layer_norm, start_rows, gain_rows[0], bias_rows[0])
    normed_low = normed_one.astype(BF16)
    grad_final = rows_in(after(cotangent, normed_low))
    joined = jnp.dot(normed_low, first_all, preferred_element_type=F32)
    queries = (joined[:, :width] + bias_rows[1]).astype(BF16).reshape(grid_shape)
    keys = joined[:, width : 2 * width].astype(BF16).reshape(grid_shape)
    values = (joined[:, 2 * width : 3 * width] + bias_rows[2]).astype(BF16).reshape(grid_shape)
    mixed, logs = attend_forward(queries, keys, values, H)
    mixed_flat = mixed.reshape(row_total, width)
    middle = start_rows + (jnp.dot(mixed_flat, full_out, preferred_element_type=F32) + bias_rows[3])
    normed_two, norm_pull_two = jax.vjp(layer_norm, middle, gain_rows[1], bias_rows[4])
    second_low = normed_two.astype(BF16)
    upper_rows = jnp.dot(second_low, full_up, preferred_element_type=F32) + up_shift
    active, gelu_pull = jax.vjp(exact_gelu, upper_rows)
    active_low = active.astype(BF16)

    def by_owner(part):
        return part.reshape(devices, -1, part.shape[1])

    down_sum = Reduction(by_owner(dot(active_low, grad_final, 0, 0)))
    sent = down_sum.send()
    (grad_final_b,) = (after(grad_final, *sent),)
    grad_active = dot(grad_final_b, full_down, 1, 1)
    (grad_upper,) = gelu_pull(grad_active)
    grad_upper_low = grad_upper.astype(BF16)
    down_sum.add(grad_upper_low)
    sent = down_sum.send()
    up_sum = Reduction(by_owner(dot(after(second_low, *sent), grad_upper_low, 0, 0)))
    sent = up_sum.send()
    grad_up_shift = jnp.sum(grad_upper_low.astype(F32), axis=0)
    grad_second = dot(after(grad_upper_low, *sent), full_up, 1, 1)
    grad_mid_norm, grad_gain_two, grad_bias_two = norm_pull_two(grad_second)
    grad_middle = grad_final.astype(F32) + grad_mid_norm
    grad_branch = grad_middle.astype(BF16)
    up_sum.add(grad_branch)
    sent = up_sum.send()
    out_sum = Reduction(by_owner(dot(mixed_flat, after(grad_branch, *sent), 0, 0)))
    sent = out_sum.send()
    grad_out_bias = jnp.sum(grad_branch.astype(F32), axis=0)
    grad_mixed = dot(after(grad_branch, *sent), full_out, 1, 1).astype(BF16).reshape(grid_shape)
    final_rows = middle + (jnp.dot(active_low, full_down, preferred_element_type=F32) + bias_rows[5])
    activations = rows_out(after(final_rows.astype(BF16), grad_mixed))

    groups = 2
    per_group = width // 128 // groups
    group_width = width // groups
    qkv_sums, joined_pieces = [], []
    for g in range(groups):
        piece = attend_backward(queries, keys, values, grad_mixed, logs, H, g * per_group, per_group)
        piece = jnp.concatenate([p.reshape(row_total, -1) for p in piece], axis=1)
        joined_pieces.append(piece)
        if g == 0:
            out_sum.add(piece)
            sent = out_sum.send()
            down_sum.add(piece)
            sent += down_sum.send()
            qkv_sums.append(Reduction(by_owner(dot(after(normed_low, *sent), piece, 0, 0))))
            sent = qkv_sums[0].send()
            grad_mixed = after(grad_mixed, *sent)
        else:
            up_sum.add(piece)
            sent = up_sum.send()
            qkv_sums[0].add(piece)
            sent += qkv_sums[0].send()
            qkv_sums.append(Reduction(by_owner(dot(after(normed_low, *sent), piece, 0, 0))))
            sent = qkv_sums[1].send()
    grad_first = 0.0
    for g in range(groups):
        cols = [slice(i * width + g * group_width, i * width + (g + 1) * group_width) for i in range(3)]
        weight = jnp.concatenate([full_qkv[:, c] for c in cols], axis=1)
        grad_first = grad_first + dot(after(joined_pieces[g], *sent), weight, 1, 1)
    grad_query_bias = jnp.concatenate(
        [jnp.sum(p[:, :group_width].astype(F32), axis=0) for p in joined_pieces]
    )
    grad_value_bias = jnp.concatenate(
        [jnp.sum(p[:, 2 * group_width :].astype(F32), axis=0) for p in joined_pieces]
    )
    grad_start_norm, grad_gain_one, grad_bias_one = norm_pull_one(grad_first)
    grad_start = grad_middle + grad_start_norm
    input_low = jnp.where(masked, 0.0, grad_start).astype(BF16)
    qkv_sums[1].add(input_low)
    qkv_sums[1].send()
    input_grad = rows_out(input_low)
    grad_mask_part = jnp.sum(jnp.where(masked, grad_start, 0.0), axis=0)
    grad_down_bias = jnp.sum(grad_final.astype(F32), axis=0)
    small_grads = jnp.stack(
        [
            grad_mask_part,
            grad_gain_one,
            grad_gain_two,
            grad_bias_one,
            grad_query_bias,
            grad_value_bias,
            grad_out_bias,
            grad_bias_two,
            grad_down_bias,
        ]
    )
    up_rows = grad_up_shift.reshape(devices, spread, share).transpose(1, 0, 2).reshape(spread, width)
    small_grads = jnp.concatenate([small_grads, up_rows], axis=0)
    small_grads = jnp.pad(small_grads, ((0, 128 - 9 - spread), (0, 0))).T
    small_sum = Reduction(by_owner(small_grads), F32)
    small_sum.send()
    for rest in (down_sum, out_sum, up_sum, qkv_sums[0], qkv_sums[1], small_sum):
        while True:
            rest.add()
            if not rest.stages:
                break
            rest.send()
    grad_down = down_sum.array.reshape(w_down.shape)
    grad_up = up_sum.array.reshape(w_up.shape)
    grad_out = out_sum.array.reshape(w_out.shape)
    pieces = [r.array.reshape(share, 3, group_width) for r in qkv_sums]
    grad_qkv = jnp.concatenate([p[:, i] for i in range(3) for p in pieces], axis=1)
    own_rows = small_sum.array.reshape(share, 128).T
    grad_up_bias = own_rows[9 : 9 + spread].reshape(-1)

    def moved(average, param):
        return 0.9 * average + 0.1 * param.astype(F32)

    return (
        activations,
        input_grad,
        grad_qkv,
        grad_out,
        own_rows[0],
        own_rows[1:3],
        own_rows[3:9],
        grad_up,
        grad_down,
        grad_up_bias,
        moved(avg_qkv, w_qkv),
        moved(avg_out, w_out),
        moved(avg_mask, mask_embed),
        moved(avg_gains, gains),
        moved(avg_biases, biases),
        moved(avg_up, w_up),
        moved(avg_down, w_down),
        moved(avg_up_bias, up_bias),
    )


def solution(mesh):
    seq_size, clip_size = mesh.shape["seq"], mesh.shape["clip"]
    fine = Mesh(mesh.devices.reshape(seq_size // 2, 2, clip_size), ALL)
    rows = P("clip", None, ("sx", "core"), None)
    first, second, only = P(ALL, None), P(None, ALL), P(ALL)
    params = (first, first, only, second, second, first, first, only)
    return jax.shard_map(
        body,
        mesh=fine,
        in_specs=(rows, P("clip", None), P("clip"), rows) + params + params,
        out_specs=(rows, rows) + params + params,
        check_vma=False,
    )
```

```python
import math
from functools import partial

import jax
import jax.numpy as jnp
from jax import lax
from jax.experimental import pallas as pl
from jax.experimental.pallas import tpu as pltpu
from jax.sharding import Mesh, PartitionSpec as P

H = 12
norm_eps = 1e-06
F32 = jnp.float32
BF16 = jnp.bfloat16
ALL = ("sx", "core", "clip")


def layer_norm(hidden, gain_row, shift_row):
    center = hidden - jnp.mean(hidden, axis=-1, keepdims=True)
    spread = jnp.mean(center * center, axis=-1, keepdims=True)
    return center * lax.rsqrt(spread + norm_eps) * gain_row + shift_row


def dot(left_side, right_side, left_dim, right_dim):
    return lax.dot_general(
        left_side, right_side, (((left_dim,), (right_dim,)), ((), ())), preferred_element_type=F32
    )


def load_rows(ref):
    return ref[...].reshape(ref.shape[0] * ref.shape[2], ref.shape[3])


def forward_kernel(q_ref, k_ref, v_ref, o_ref, log_ref, *, head_size, scale):
    query, key, value = load_rows(q_ref) * scale, load_rows(k_ref), load_rows(v_ref)
    mixed = []
    for i in range(query.shape[1] // head_size):
        cols = slice(i * head_size, (i + 1) * head_size)
        scores = dot(key[:, cols], query[:, cols], 1, 1)
        top = jnp.max(scores, axis=0, keepdims=True)
        shifted = jnp.exp(scores - top)
        total = jnp.sum(shifted, axis=0, keepdims=True)
        mixed.append(dot(value[:, cols], shifted.astype(BF16), 0, 0) / total)
        log_ref[0, 0, i : i + 1, :] = top + jnp.log(total)
    mixed = jnp.concatenate(mixed, axis=0).T.astype(BF16)
    o_ref[...] = mixed.reshape(o_ref.shape)


def backward_kernel(q_ref, k_ref, v_ref, g_ref, log_ref, d_ref, *, head_size, scale):
    query, key, value = load_rows(q_ref) * scale, load_rows(k_ref), load_rows(v_ref)
    grad = load_rows(g_ref)
    grad_query, grad_key, grad_value = [], [], []
    for i in range(query.shape[1] // head_size):
        cols = slice(i * head_size, (i + 1) * head_size)
        scores = dot(key[:, cols], query[:, cols], 1, 1)
        prob = jnp.exp(scores - log_ref[0, 0, i : i + 1, :])
        grad_prob = dot(value[:, cols], grad[:, cols], 1, 1)
        inner = jnp.sum(grad_prob * prob, axis=0, keepdims=True)
        grad_scores = (prob * (grad_prob - inner)).astype(BF16)
        grad_query.append(dot(key[:, cols], grad_scores, 0, 0))
        grad_key.append(dot(grad_scores, query[:, cols], 1, 0))
        grad_value.append(dot(prob.astype(BF16), grad[:, cols], 1, 0))
    rows = d_ref.shape[:3]
    wide = query.shape[1]
    dq = (jnp.concatenate(grad_query, axis=0) * scale).T.astype(BF16)
    d_ref[..., :wide] = dq.reshape(rows + (wide,))
    d_ref[..., wide : 2 * wide] = jnp.concatenate(grad_key, axis=1).astype(BF16).reshape(rows + (wide,))
    d_ref[..., 2 * wide :] = jnp.concatenate(grad_value, axis=1).astype(BF16).reshape(rows + (wide,))


PAIR = 128


def pair_spec(grid_shape, first, wide=PAIR):
    slots, _, rows, _ = grid_shape
    return pl.BlockSpec((slots, 1, rows, wide), lambda c, j: (0, c, 0, j + first))


def attend_forward(joined, grid_shape, head_count):
    slots, clips, rows, width = grid_shape
    head_size = width // head_count
    blocks, per_block = width // PAIR, PAIR // head_size
    return pl.pallas_call(
        partial(forward_kernel, head_size=head_size, scale=1.0 / math.sqrt(head_size)),
        grid=(clips, blocks),
        in_specs=[pair_spec(grid_shape, i * blocks) for i in range(3)],
        out_specs=[
            pair_spec(grid_shape, 0),
            pl.BlockSpec((1, 1, per_block, slots * rows), lambda c, j: (c, j, 0, 0)),
        ],
        out_shape=[
            jax.ShapeDtypeStruct(grid_shape, BF16),
            jax.ShapeDtypeStruct((clips, blocks, per_block, slots * rows), F32),
        ],
        name="attend_forward",
    )(joined, joined, joined)


def attend_backward(joined, grad_mixed, logs, head_count, first, count):
    slots, clips, rows, width = grid_shape = grad_mixed.shape
    head_size = width // head_count
    per_block = PAIR // head_size
    return pl.pallas_call(
        partial(backward_kernel, head_size=head_size, scale=1.0 / math.sqrt(head_size)),
        grid=(clips, count),
        in_specs=[pair_spec(grid_shape, i * (width // PAIR) + first) for i in range(3)]
        + [
            pair_spec(grid_shape, first),
            pl.BlockSpec((1, 1, per_block, slots * rows), lambda c, j: (c, j + first, 0, 0)),
        ],
        out_specs=pair_spec(grid_shape, 0, 3 * PAIR),
        out_shape=jax.ShapeDtypeStruct((slots, clips, rows, count * 3 * PAIR), BF16),
        name="attend_backward",
    )(joined, joined, joined, grad_mixed, logs)


def first_kernel(one_ref, two_ref, q_ref, k_ref, v_ref, grad_ref):
    weights = (q_ref, k_ref, v_ref)
    cols = [slice(c, c + PAIR) for c in range(0, q_ref.shape[1], PAIR)]
    weight = jnp.concatenate([ref[:, c] for c in cols for ref in weights], axis=1)
    cut = one_ref.shape[1]
    grad_ref[...] = dot(one_ref[...], weight[:, :cut], 1, 1) + dot(two_ref[...], weight[:, cut:], 1, 1)


def feed_first(piece_one, piece_two, w_qkv):
    rows, width = piece_one.shape[0], w_qkv.shape[0]
    tile = rows // 2
    return pl.pallas_call(
        first_kernel,
        grid=(rows // tile,),
        in_specs=[pl.BlockSpec((tile, p.shape[1]), lambda r: (r, 0)) for p in (piece_one, piece_two)]
        + [pl.BlockSpec((width, width), lambda r, i=i: (0, i)) for i in range(3)],
        out_specs=pl.BlockSpec((tile, width), lambda r: (r, 0)),
        out_shape=jax.ShapeDtypeStruct((rows, width), F32),
        name="feed_first",
    )(piece_one, piece_two, w_qkv, w_qkv, w_qkv)


def order_kernel(one_ref, two_ref, out_ref):
    joined = jnp.concatenate([one_ref[...], two_ref[...]], axis=1)
    pairs = joined.shape[1] // (3 * PAIR)
    for i in range(3):
        for p in range(pairs):
            to, at = i * pairs + p, 3 * p + i
            out_ref[:, to * PAIR : (to + 1) * PAIR] = joined[:, at * PAIR : (at + 1) * PAIR]


def natural_order(one, two):
    shape = (one.shape[0], one.shape[1] + two.shape[1])
    return pl.pallas_call(order_kernel, out_shape=jax.ShapeDtypeStruct(shape, F32), name="natural_order")(one, two)


DOWN_ROWS = 96
HIDDEN = 8 * DOWN_ROWS
CHUNK = 256


def up_kernel(second_ref, w_ref, bias_ref, cot_ref, active_ref, slope_ref, grad_ref):
    total = 0.0
    for r in range(0, second_ref.shape[0], CHUNK):
        rows = slice(r, r + CHUNK)
        upper = dot(second_ref[rows, :], w_ref[...], 1, 0) + bias_ref[...]
        below = 0.5 + 0.5 * lax.erf(upper * math.sqrt(0.5))
        bell = jnp.exp(upper * upper * -0.5) * (1.0 / math.sqrt(2.0 * math.pi))
        active = (upper * below).astype(BF16)
        active_ref[rows, :] = active
        slope_ref[rows, :] = below + upper * bell
        total = total + dot(active, cot_ref[rows, :], 0, 0)
    grad_ref[...] = total.astype(BF16)


def down_spec(w_down):
    return pl.BlockSpec((HIDDEN // DOWN_ROWS, DOWN_ROWS, w_down.shape[2]), lambda j: (j, 0, 0))


def feed_up(second, w_up, bias, cot):
    rows, width = second.shape
    hidden = bias.shape[1]
    whole = pl.BlockSpec((rows, width), lambda j: (0, 0))
    tall = pl.BlockSpec((rows, HIDDEN), lambda j: (0, j))
    return pl.pallas_call(
        up_kernel,
        grid=(hidden // HIDDEN,),
        in_specs=[
            whole,
            pl.BlockSpec((width, HIDDEN), lambda j: (0, j)),
            pl.BlockSpec((1, HIDDEN), lambda j: (0, j)),
            whole,
        ],
        out_specs=[tall, tall, pl.BlockSpec((HIDDEN, width), lambda j: (j, 0))],
        out_shape=[
            jax.ShapeDtypeStruct((rows, hidden), BF16),
            jax.ShapeDtypeStruct((rows, hidden), F32),
            jax.ShapeDtypeStruct((hidden, width), BF16),
        ],
        name="feed_up",
    )(second, w_up, bias, cot)


def final_kernel(active_ref, w_ref, middle_ref, bias_ref, out_ref):
    weight = w_ref[...].reshape(active_ref.shape[1], -1)
    total = dot(active_ref[...], weight, 1, 0) + bias_ref[...]
    out_ref[...] = (middle_ref[...] + total).astype(BF16)


def feed_final(active, w_down, middle, bias):
    rows, width = middle.shape
    hidden = active.shape[1]
    return pl.pallas_call(
        final_kernel,
        grid=(rows // CHUNK,),
        in_specs=[
            pl.BlockSpec((CHUNK, hidden), lambda r: (r, 0)),
            pl.BlockSpec((hidden // DOWN_ROWS, DOWN_ROWS, width), lambda r: (0, 0, 0)),
            pl.BlockSpec((CHUNK, width), lambda r: (r, 0)),
            pl.BlockSpec((1, width), lambda r: (0, 0)),
        ],
        out_specs=pl.BlockSpec((CHUNK, width), lambda r: (r, 0)),
        out_shape=jax.ShapeDtypeStruct((rows, width), BF16),
        name="feed_final",
    )(active, w_down, middle, bias)


def back_kernel(second_ref, cot_ref, w_up_ref, w_down_ref, slope_ref, grad_up_ref, bias_ref, grad_ref):
    @pl.when(pl.program_id(0) == 0)
    def _():
        grad_ref[...] = jnp.zeros_like(grad_ref)

    w_down = w_down_ref[...].reshape(HIDDEN, -1)
    total, column = 0.0, 0.0
    for r in range(0, second_ref.shape[0], CHUNK):
        rows = slice(r, r + CHUNK)
        upper = dot(cot_ref[rows, :], w_down, 1, 1) * slope_ref[rows, :]
        upper = upper.astype(BF16)
        column = column + jnp.sum(upper.astype(F32), axis=0, keepdims=True)
        grad_ref[rows, :] += dot(upper, w_up_ref[...], 1, 1)
        total = total + dot(second_ref[rows, :], upper, 0, 0)
    grad_up_ref[...] = total.astype(BF16)
    bias_ref[...] = column


def feed_back(second, cot, w_up, w_down, slope):
    rows, width = second.shape
    hidden = slope.shape[1]
    whole = pl.BlockSpec((rows, width), lambda j: (0, 0))
    return pl.pallas_call(
        back_kernel,
        grid=(hidden // HIDDEN,),
        in_specs=[
            whole,
            whole,
            pl.BlockSpec((width, HIDDEN), lambda j: (0, j)),
            down_spec(w_down),
            pl.BlockSpec((rows, HIDDEN), lambda j: (0, j)),
        ],
        out_specs=[
            pl.BlockSpec((width, HIDDEN), lambda j: (0, j)),
            pl.BlockSpec((1, HIDDEN), lambda j: (0, j)),
            whole,
        ],
        out_shape=[
            jax.ShapeDtypeStruct((width, hidden), BF16),
            jax.ShapeDtypeStruct((1, hidden), F32),
            jax.ShapeDtypeStruct((rows, width), F32),
        ],
        name="feed_back",
    )(second, cot, w_up, w_down, slope)


def after(array, *earlier):
    return lax.optimization_barrier((array,) + earlier)[0]


def device_bits():
    bits = []
    for axis_name in ALL:
        bit = lax.axis_size(axis_name) // 2
        while bit:
            bits.append((axis_name, bit))
            bit //= 2
    return bits


def make_stages(bits, form="direct"):
    core = [b for b in bits if b[0] == "core"]
    across = [b for b in bits if b[0] == "sx"]
    clip = [b for b in bits if b[0] == "clip"][::-1]
    plane = {"direct": [across + clip[:1]], "x": [across, clip[:1]], "y": [clip[:1], across]}[form]
    stages = [core] + plane + [clip[i : i + 2] for i in range(1, len(clip), 2)]
    return [sorted(stage, key=bits.index) for stage in stages if stage]


def partners(stage):
    count = len(stage)
    return [[(k >> i) & 1 for i in range(count)] for k in range(1, 1 << count)]


def send_to(array, stage, flags):
    axes = tuple(dict.fromkeys(step[0] for step in stage))
    sizes = [lax.axis_size(name) for name in axes]
    flip = [sum(s[1] for s, f in zip(stage, flags) if f and s[0] == name) for name in axes]
    total = math.prod(sizes)
    if len(axes) == 1:
        return lax.ppermute(array, axes[0], [(i, i ^ flip[0]) for i in range(total)])
    pairs = [(i, (i // sizes[1] ^ flip[0]) * sizes[1] + (i % sizes[1] ^ flip[1])) for i in range(total)]
    return lax.ppermute(array, axes, pairs)


def own_bit(step):
    return (lax.axis_index(step[0]) // step[1]) % 2


class Reduction:
    def __init__(self, parts, form="direct", send_type=BF16):
        self.left = device_bits()
        self.stages = make_stages(self.left, form)
        self.arrays = [part.reshape((2,) * len(self.left) + part.shape[1:]) for part in parts]
        self.send_type = send_type

    def pick(self, array, stage, flags):
        left = list(self.left)
        for step, flag in zip(stage, flags):
            axis = left.index(step)
            array = lax.dynamic_index_in_dim(array, own_bit(step) ^ flag, axis, False)
            left.pop(axis)
        return array

    def send(self):
        stage = self.stages.pop(0)
        sent = []
        for flags in partners(stage):
            picked = [self.pick(a, stage, flags).astype(self.send_type) for a in self.arrays]
            sent.append(picked[0] if len(picked) == 1 else jnp.concatenate(picked, axis=-1))
        self.arrays = [self.pick(a, stage, [0] * len(stage)) for a in self.arrays]
        self.left = [step for step in self.left if step not in stage]
        self.got = [send_to(array, stage, f) for array, f in zip(sent, partners(stage))]
        return sent

    def add(self, *earlier):
        got = self.got
        if earlier:
            got = lax.optimization_barrier(tuple(got) + earlier)[: len(got)]
        first = 0
        for i, array in enumerate(self.arrays):
            last = first + array.shape[-1]
            array = array.astype(F32)
            for piece in got:
                array = array + piece[..., first:last].astype(F32)
            self.arrays[i] = array
            first = last


def gather_all(shard, *earlier):
    bits = device_bits()
    array, have = shard, []
    for stage in make_stages(bits)[::-1]:
        if earlier and stage[0][0] == "core":
            array = after(array, *earlier)
        blocks = [([0] * len(stage), array)]
        blocks += [(f, send_to(array, stage, f)) for f in partners(stage)]
        have = sorted(have + stage, key=bits.index)
        axes = [have.index(step) for step in stage]
        array = jnp.expand_dims(array, axes)
        shape = tuple(2 if i in axes else 1 for i in range(array.ndim))
        for flags, block in blocks[1:]:
            here = jnp.full(shape, True)
            for step, flag, axis in zip(stage, flags, axes):
                here &= lax.broadcasted_iota(jnp.int32, shape, axis) == (own_bit(step) ^ flag)
            array = jnp.where(here, jnp.expand_dims(block, axes), array)
    return array.reshape((-1,) + shard.shape)


def body(
    patches,
    mask_index,
    mask_count,
    cotangent,
    w_qkv,
    w_out,
    mask_embed,
    gains,
    biases,
    w_up,
    w_down,
    up_bias,
    avg_qkv,
    avg_out,
    avg_mask,
    avg_gains,
    avg_biases,
    avg_up,
    avg_down,
    avg_up_bias,
):
    clip_count, freq_rows, time_local, width = patches.shape
    seq_names = ("sx", "core")
    seq_size = lax.axis_size("sx") * lax.axis_size("core")
    seq_here = lax.axis_index(seq_names)
    devices = seq_size * lax.axis_size("clip")
    local_len = freq_rows * time_local
    own_clips = clip_count // seq_size
    row_total = seq_size * own_clips * local_len
    grid_shape = (seq_size, own_clips, local_len, width)

    def trade(chunks):
        return [chunks[0]] + [
            lax.ppermute(chunks[k], seq_names, [(i, i ^ k) for i in range(seq_size)])
            for k in range(1, seq_size)
        ]

    def rows_in(array):
        array = array.reshape(seq_size, own_clips, local_len, width)
        return trade([lax.dynamic_index_in_dim(array, seq_here ^ k, 0, False) for k in range(seq_size)])

    def rows_out(array):
        array = array.reshape(grid_shape)
        return trade([array[k] for k in range(seq_size)])

    def in_place(got):
        got = jnp.stack(got)
        order = [lax.dynamic_index_in_dim(got, seq_here ^ k, 0, False) for k in range(seq_size)]
        return jnp.stack(order).reshape(patches.shape)

    share = w_qkv.shape[0]
    spread = up_bias.shape[0] // share
    pairs = width // PAIR

    small = jnp.concatenate([mask_embed[None], gains, biases, up_bias.reshape(spread, share)], axis=0)
    small = jnp.pad(small, ((0, 128 - small.shape[0]), (0, 0))).T
    small_all = gather_all(small)
    patch_rows = jnp.stack(rows_in(patches)).reshape(row_total, width)
    moved_all = tuple(
        0.9 * average + 0.1 * param.astype(F32)
        for average, param in (
            (avg_qkv, w_qkv),
            (avg_out, w_out),
            (avg_mask, mask_embed),
            (avg_gains, gains),
            (avg_biases, biases),
            (avg_up, w_up),
            (avg_down, w_down),
            (avg_up_bias, up_bias),
        )
    )
    small_rows = small_all.reshape(width, -1).astype(F32).T
    mask_vector, gain_rows, bias_rows = small_rows[0], small_rows[1:3], small_rows[3:9]
    up_shift = small_rows[9 : 9 + spread].reshape(spread, devices, share)
    up_shift = up_shift.transpose(1, 0, 2).reshape(1, -1)
    joined_bias = jnp.concatenate([bias_rows[1], jnp.zeros_like(bias_rows[1]), bias_rows[2]])

    hidden = spread * width
    down_share = w_down.shape[0]
    others = [w_down] + [w_up[:, j * width : (j + 1) * width] for j in range(spread)] + [w_out]
    others_all = lax.all_gather(jnp.concatenate(others, axis=0), ALL, axis=0)

    def other_rows(block):
        first = down_share + block * share
        return others_all[:, first : first + share].reshape(width, width)

    full_up = jnp.concatenate([other_rows(j) for j in range(spread)], axis=1)
    full_out = other_rows(spread)
    if down_share == DOWN_ROWS:
        full_down = others_all
    else:
        full_down = others_all[:, :down_share].reshape(-1, DOWN_ROWS, width)

    slot_ids = lax.broadcasted_iota(jnp.int32, (seq_size, freq_rows, time_local), 0)
    freq_ids = lax.broadcasted_iota(jnp.int32, (seq_size, freq_rows, time_local), 1)
    time_ids = lax.broadcasted_iota(jnp.int32, (seq_size, freq_rows, time_local), 2)
    time_ids = time_ids + (slot_ids ^ seq_here) * time_local
    positions = (freq_ids * (time_local * seq_size) + time_ids).reshape(-1)
    own_index = lax.dynamic_slice_in_dim(mask_index, seq_here * own_clips, own_clips, 0)
    own_count = lax.dynamic_slice_in_dim(mask_count, seq_here * own_clips, own_clips, 0)
    live = lax.broadcasted_iota(jnp.int32, own_index.shape, 1) < own_count[:, None]
    live_index = jnp.where(live, own_index, -1)
    hits = live_index[:, :, None] == positions[None, None, :]
    masked = jnp.any(hits, axis=1).reshape(own_clips, seq_size, local_len)
    masked = masked.transpose(1, 0, 2).reshape(row_total, 1)

    start_rows = jnp.where(masked, mask_vector, patch_rows.astype(F32))
    normed_one, norm_pull_one = jax.vjp(layer_norm, start_rows, gain_rows[0], bias_rows[0])
    normed_low = normed_one.astype(BF16)
    full_qkv = gather_all(w_qkv, normed_low).reshape(width, -1)
    joined = (jnp.dot(normed_low, full_qkv, preferred_element_type=F32) + joined_bias).astype(BF16)
    joined = joined.reshape(grid_shape[:3] + (-1,))
    cot_parts = rows_in(after(cotangent, joined))
    mixed, logs = attend_forward(joined, grid_shape, H)
    cot_parts = lax.optimization_barrier(tuple(cot_parts) + (mixed,))[:-1]
    grad_final = jnp.stack(cot_parts).reshape(row_total, width)
    mixed_flat = mixed.reshape(row_total, width)
    middle = start_rows + (jnp.dot(mixed_flat, full_out, preferred_element_type=F32) + bias_rows[3])
    normed_two, norm_pull_two = jax.vjp(layer_norm, middle, gain_rows[1], bias_rows[4])
    second_low = normed_two.astype(BF16)

    def by_owner(part):
        return part.reshape(devices, -1, part.shape[1])

    active_low, slope, grad_down_part = feed_up(second_low, full_up, up_shift, grad_final)
    grad_down = lax.psum_scatter(grad_down_part, ALL, scatter_dimension=0, tiled=True).astype(F32)
    final_low = feed_final(active_low, full_down, middle, bias_rows[5:6])
    grad_up_part, grad_up_shift, grad_second = feed_back(second_low, grad_final, full_up, full_down, slope)
    up_sum = Reduction([by_owner(grad_up_part)])
    sent = up_sum.send()
    grad_second = after(grad_second, *sent)
    grad_mid_norm, grad_gain_two, grad_bias_two = norm_pull_two(grad_second)
    grad_middle = grad_final.astype(F32) + grad_mid_norm
    grad_branch = grad_middle.astype(BF16)
    out_sum = Reduction([by_owner(dot(mixed_flat, grad_branch, 0, 0))])
    sent = out_sum.send()
    grad_out_bias = jnp.sum(grad_branch.astype(F32), axis=0)
    grad_mixed = dot(after(grad_branch, *sent), full_out, 1, 1).astype(BF16).reshape(grid_shape)
    up_sum.add(grad_mixed)
    out_sum.add(grad_mixed)
    up_sum.arrays += out_sum.arrays
    sent = up_sum.send()
    grad_mixed = after(grad_mixed, *sent)

    half = pairs // 2
    piece_one = attend_backward(joined, grad_mixed, logs, H, 0, half).reshape(row_total, -1)
    part_one = dot(normed_low, piece_one, 0, 0)
    mid_sum = Reduction([by_owner(part_one)])
    sent = mid_sum.send()
    up_sum.add(part_one, *sent)
    sent = up_sum.send()
    activations = rows_out(after(final_low, *sent))
    mid_sum.add(*sent)
    sent = mid_sum.send()
    grad_mixed = after(grad_mixed, *sent)
    piece_two = attend_backward(joined, grad_mixed, logs, H, half, pairs - half).reshape(row_total, -1)
    part_two = dot(after(normed_low, piece_two), piece_two, 0, 0)
    last_sum = Reduction([by_owner(part_two)])
    sent = last_sum.send()
    grad_first = feed_first(piece_one, after(piece_two, *sent), full_qkv)
    last_sum.add(grad_first)
    sent = last_sum.send()
    grad_first = after(grad_first, *sent)

    def column_sums(index):
        parts = [
            piece[:, (3 * p + index) * PAIR : (3 * p + index + 1) * PAIR]
            for piece, count in ((piece_one, half), (piece_two, pairs - half))
            for p in range(count)
        ]
        return jnp.concatenate([jnp.sum(part.astype(F32), axis=0) for part in parts])

    grad_query_bias = column_sums(0)
    grad_value_bias = column_sums(2)
    grad_start_norm, grad_gain_one, grad_bias_one = norm_pull_one(grad_first)
    grad_start = grad_middle + grad_start_norm
    input_low = jnp.where(masked, 0.0, grad_start).astype(BF16)
    input_grad = rows_out(input_low)
    activations = in_place(lax.optimization_barrier(tuple(activations) + (input_low,))[:-1])
    grad_mask_part = jnp.sum(jnp.where(masked, grad_start, 0.0), axis=0)
    grad_down_bias = jnp.sum(grad_final.astype(F32), axis=0)
    small_grads = jnp.stack(
        [
            grad_mask_part,
            grad_gain_one,
            grad_gain_two,
            grad_bias_one,
            grad_query_bias,
            grad_value_bias,
            grad_out_bias,
            grad_bias_two,
            grad_down_bias,
        ]
    )
    up_rows = grad_up_shift.reshape(devices, spread, share).transpose(1, 0, 2).reshape(spread, width)
    small_grads = jnp.concatenate([small_grads, up_rows], axis=0)
    small_grads = jnp.pad(small_grads, ((0, 128 - 9 - spread), (0, 0))).T
    small_sum = Reduction([by_owner(small_grads)], send_type=F32)
    small_sum.send()
    up_sum.add(input_low)
    mid_sum.add(input_low)
    small_sum.add(input_low)
    small_sum.send()
    last_sum.add(small_grads)
    small_sum.add()
    last_sum.arrays = mid_sum.arrays + last_sum.arrays + small_sum.arrays
    last_sum.send()
    last_sum.add()
    input_grad = in_place(input_grad)
    for reduction in (up_sum, last_sum):
        while reduction.stages:
            reduction.send()
            reduction.add()
    grad_up = up_sum.arrays[0]
    grad_out = up_sum.arrays[1]
    grad_qkv = natural_order(last_sum.arrays[0], last_sum.arrays[1])
    own_rows = last_sum.arrays[2].T
    grad_up_bias = own_rows[9 : 9 + spread].reshape(-1)

    return (
        activations,
        input_grad,
        grad_qkv,
        grad_out,
        own_rows[0],
        own_rows[1:3],
        own_rows[3:9],
        grad_up,
        grad_down,
        grad_up_bias,
    ) + moved_all


def solution(mesh):
    seq_size, clip_size = mesh.shape["seq"], mesh.shape["clip"]
    fine = Mesh(mesh.devices.reshape(seq_size // 2, 2, clip_size), ALL)
    rows = P("clip", None, ("sx", "core"), None)
    first, second, only = P(ALL, None), P(None, ALL), P(ALL)
    params = (first, first, only, second, second, first, first, only)
    return jax.shard_map(
        body,
        mesh=fine,
        in_specs=(rows, P("clip", None), P("clip"), rows) + params + params,
        out_specs=(rows, rows) + params + params,
        check_vma=False,
    )
```
